32 devices in a mesh: dp: 2 (over x), tm: 4 (over y, core), height: 4 (over z).
Axes of the slice: x: 2, y: 2, z: 4, core: 2. Of those that a mesh axis runs over, the one named last changes fastest.
Arguments:
- frames_in: bfloat16 [2, 12, 12, 320, 128], P('dp', 'tm', 'height'), may hold values from -6 to 6
- grad_out: bfloat16 [2, 12, 12, 320, 128], P('dp', 'tm', 'height'), may hold values from -6 to 6
- w_spatial: bfloat16 [3, 3, 128, 128], replicated, may hold values from -0.1875 to 0.1875
- w_temporal: bfloat16 [3, 128, 128], replicated, may hold values from -0.3125 to 0.3125
Outputs:
- layer_out: bfloat16 [2, 12, 12, 320, 128], P('dp', 'tm', 'height')
- grad_in: bfloat16 [2, 12, 12, 320, 128], P('dp', 'tm', 'height')
- grad_spatial: float32 [3, 3, 128, 128], replicated
- grad_temporal: float32 [3, 128, 128], replicated
The draws below stay inside these ranges and needn't reach their ends.
All inputs are finite; a program needn't handle non-finite values.
Results may differ from the reference program's by a relative error of at most 0.005.
Values may be sent and summed in bfloat16 or wider, within the bound.
A program may use at most 64 MiB of HBM per device.

```python
import math
import jax
import jax.numpy as jnp
from jax import lax

C = 128
COLS = 320
CLIPS = 2
FRAMES = 12
ROWS = 12
PIXELS = 92160


def levels(stream_key, shape, shards, low, high):
    def one(dim, blocks):
        steps = jax.random.uniform(jax.random.fold_in(jax.random.fold_in(stream_key, 6), dim), (blocks,), jnp.float32, low / len(shards), high / len(shards))
        return jnp.repeat(jnp.exp(steps), shape[dim] // blocks).reshape((-1,) + (1,) * (len(shape) - dim - 1))

    loudness = one(*shards[0])
    for cut in shards[1:]:
        loudness = loudness * one(*cut)
    return loudness


def centred(rng, shape, width, reach, shards=(), held_as=jnp.bfloat16):
    array = jax.random.normal(rng, shape, jnp.float32) * width
    if len(shards) > 0:
        array = levels(rng, shape, shards, -0.22, 0.18) * array
    return jnp.clip(array, min=-reach, max=reach).astype(held_as)


def setup_inputs(seed: int = 0) -> dict:
    streams_of = jax.random.split(jax.random.key(seed), 5)
    frames_in = centred(streams_of[0], (CLIPS, FRAMES, ROWS, COLS, C), 1.0, 6.0, ((0, 2), (1, 4), (2, 4)))
    grad_out = centred(streams_of[1], (CLIPS, FRAMES, ROWS, COLS, C), 1.0, 6.0, ((0, 2), (1, 4), (2, 4)))
    w_spatial = centred(streams_of[2], (3, 3, C, C), (9 * C) ** -0.5, 0.1875)
    w_temporal = centred(streams_of[3], (3, C, C), (3 * C) ** -0.5, 0.3125)
    return {"frames_in": frames_in, "grad_out": grad_out, "w_spatial": w_spatial, "w_temporal": w_temporal}


def reference(frames_in, grad_out, w_spatial, w_temporal):
    spatial_f = w_spatial.astype(jnp.float32)
    temporal_f = w_temporal.astype(jnp.float32)

    def clip_step(carry, pair):
        clip_x, clip_g = pair
        padded_x = jnp.pad(clip_x, ((0, 0), (1, 1), (1, 1), (0, 0))).astype(jnp.float32)
        pre_act = jnp.zeros((FRAMES, ROWS, COLS, C), jnp.float32)
        for row_tap in range(3):
            for col_tap in range(3):
                pre_act = pre_act + jnp.einsum('frwc,cd->frwd', padded_x[:, row_tap:row_tap + ROWS, col_tap:col_tap + COLS], spatial_f[row_tap, col_tap])
        hidden = jax.nn.silu(pre_act).astype(jnp.bfloat16)
        hidden_pad = jnp.pad(hidden, ((2, 0), (0, 0), (0, 0), (0, 0))).astype(jnp.float32)
        mixed = jnp.zeros((FRAMES, ROWS, COLS, C), jnp.float32)
        for lag_tap in range(3):
            mixed = mixed + jnp.einsum('frwc,cd->frwd', hidden_pad[2 - lag_tap:2 - lag_tap + FRAMES], temporal_f[lag_tap])
        grad_full = clip_g.astype(jnp.float32)
        grad_pad = jnp.pad(grad_full, ((0, 2), (0, 0), (0, 0), (0, 0)))
        grad_hidden = jnp.zeros((FRAMES, ROWS, COLS, C), jnp.float32)
        for lag_tap in range(3):
            grad_hidden = grad_hidden + jnp.einsum('frwd,cd->frwc', grad_pad[lag_tap:lag_tap + FRAMES], temporal_f[lag_tap])
        temporal_part = jnp.stack([jnp.einsum('frwc,frwd->cd', hidden_pad[2 - lag_tap:2 - lag_tap + FRAMES], grad_full) for lag_tap in range(3)])
        sigma = jax.nn.sigmoid(pre_act)
        grad_pre = (grad_hidden * sigma * (1.0 + pre_act * (1.0 - sigma))).astype(jnp.bfloat16)
        grad_pre_f = grad_pre.astype(jnp.float32)
        grad_pre_pad = jnp.pad(grad_pre_f, ((0, 0), (1, 1), (1, 1), (0, 0)))
        grad_input = jnp.zeros((FRAMES, ROWS, COLS, C), jnp.float32)
        for row_tap in range(3):
            for col_tap in range(3):
                grad_input = grad_input + jnp.einsum('frwd,cd->frwc', grad_pre_pad[:, 2 - row_tap:2 - row_tap + ROWS, 2 - col_tap:2 - col_tap + COLS], spatial_f[row_tap, col_tap])
        spatial_part = jnp.stack([jnp.stack([jnp.einsum('frwc,frwd->cd', padded_x[:, row_tap:row_tap + ROWS, col_tap:col_tap + COLS], grad_pre_f) for col_tap in range(3)]) for row_tap in range(3)])
        new_carry = (carry[0] + spatial_part, carry[1] + temporal_part)
        return (new_carry, (mixed.astype(jnp.bfloat16), grad_input.astype(jnp.bfloat16)))
    start = (jnp.zeros((3, 3, C, C), jnp.float32), jnp.zeros((3, C, C), jnp.float32))
    sums, outputs = lax.scan(clip_step, start, (frames_in, grad_out))
    factor = 1.0 / math.sqrt(PIXELS)
    return (outputs[0], outputs[1], sums[0] * factor, sums[1] * factor)
```

```python
import functools
import math

import jax
import jax.numpy as jnp
from jax import lax
from jax.experimental import pallas as pl
from jax.experimental.pallas import tpu as pltpu
from jax.sharding import PartitionSpec as P

F32, BF16 = jnp.float32, jnp.bfloat16


def tdot(lhs, rhs):
    return lax.dot_general(lhs, rhs, (((0,), (0,)), ((), ())), preferred_element_type=F32)


def dot(lhs, rhs):
    return jnp.dot(lhs, rhs, preferred_element_type=F32)


def kernel(
    sizes, dims, factor,
    x_hbm, g_hbm, ws_ref, wt_ref,
    lo_hbm, gi_hbm, res_hbm,
    x_ext, xs, g_ext, hid, gp, gps, wb, wtb, acc, part, rs1, s1, rs2, dps, res, lo, gi,
    loc, xh_s, xh_r, gh_s, gh_r, hd_s, hd_r, gp_s, gp_r,
    rs1_s, rs1_r, rs2_s, rs2_r, dp_s, dp_r, ag1_s, ag1_r, ag2_s, ag2_r,
):
    n_dp, n_tm, n_h = sizes
    frames, rows, cols, ch = dims
    pix = rows * cols
    total = 12 * ch
    chunk = total // n_tm
    piece = chunk // n_h
    spatial_chunks = (9 * ch) // chunk
    me_dp, me_tm, me_h = lax.axis_index("dp"), lax.axis_index("tm"), lax.axis_index("height")

    def remote(src, dst, send, recv, axis, peer):
        return pltpu.make_async_remote_copy(
            src_ref=src, dst_ref=dst, send_sem=send, recv_sem=recv,
            device_id={axis: peer}, device_id_type=pl.DeviceIdType.MESH,
        )

    x_in = pltpu.make_async_copy(x_hbm.at[0], x_ext.at[:, pl.ds(1, rows)], loc.at[0])
    g_in = pltpu.make_async_copy(g_hbm.at[0], g_ext.at[pl.ds(0, frames)], loc.at[1])
    x_in.start()
    g_in.start()

    barrier = pltpu.get_barrier_semaphore()
    axes = (("dp", n_dp, me_dp), ("tm", n_tm, me_tm), ("height", n_h, me_h))
    for axis, count, me in axes:
        for step in range(1, count):
            pl.semaphore_signal(
                barrier, inc=1, device_id={axis: lax.rem(me + step, count)},
                device_id_type=pl.DeviceIdType.MESH,
            )
    pl.semaphore_wait(barrier, n_dp + n_tm + n_h - 3)

    has_up, has_down = me_h > 0, me_h < n_h - 1
    has_prev, has_next = me_tm > 0, me_tm < n_tm - 1
    up, down = lax.rem(me_h + n_h - 1, n_h), lax.rem(me_h + 1, n_h)
    prev, nxt = lax.rem(me_tm + n_tm - 1, n_tm), lax.rem(me_tm + 1, n_tm)

    x_down = remote(x_hbm.at[0, :, rows - 1], x_ext.at[:, 0], xh_s.at[0], xh_r.at[0], "height", down)
    x_up = remote(x_hbm.at[0, :, 0], x_ext.at[:, rows + 1], xh_s.at[1], xh_r.at[1], "height", up)
    g_prev = remote(
        g_hbm.at[0, pl.ds(0, 2)], g_ext.at[pl.ds(frames, 2)], gh_s.at[0], gh_r.at[0], "tm", prev
    )
    pl.when(has_down)(x_down.start)
    pl.when(has_up)(x_up.start)
    pl.when(has_prev)(g_prev.start)

    @pl.when(me_h == 0)
    def _():
        x_ext[:, 0] = jnp.zeros((frames, cols, ch), BF16)
        gp[:, 0] = jnp.zeros((frames, cols, ch), BF16)

    @pl.when(me_h == n_h - 1)
    def _():
        x_ext[:, rows + 1] = jnp.zeros((frames, cols, ch), BF16)
        gp[:, rows + 1] = jnp.zeros((frames, cols, ch), BF16)

    @pl.when(me_tm == 0)
    def _():
        hid[pl.ds(0, 2)] = jnp.zeros((2, rows, cols, ch), BF16)

    @pl.when(me_tm == n_tm - 1)
    def _():
        g_ext[pl.ds(frames, 2)] = jnp.zeros((2, rows, cols, ch), BF16)

    for i in range(3):
        for j in range(3):
            wb[i, pl.ds((2 - j) * ch, ch)] = ws_ref[i, j].T
        wtb[pl.ds(i * ch, ch)] = wt_ref[i].T

    place = lax.broadcasted_iota(jnp.int32, (cols, ch), 0)

    def stack(source, target, f, r):
        value = source[f, r]
        wide = value.astype(F32)
        left = jnp.where(place == 0, 0.0, pltpu.roll(wide, 1, 0))
        right = jnp.where(place == cols - 1, 0.0, pltpu.roll(wide, cols - 1, 0))
        target[f, r, :, pl.ds(0, ch)] = left.astype(BF16)
        target[f, r, :, pl.ds(ch, ch)] = value
        target[f, r, :, pl.ds(2 * ch, ch)] = right.astype(BF16)

    x_in.wait()

    @pl.loop(0, frames)
    def _(f):
        for r in range(1, rows + 1):
            stack(x_ext, xs, f, r)

    g_in.wait()
    pl.when(has_up)(x_down.wait_recv)
    pl.when(has_down)(x_up.wait_recv)

    @pl.loop(0, frames)
    def _(f):
        for r in (0, rows + 1):
            stack(x_ext, xs, f, r)

    pl.when(has_next)(g_prev.wait_recv)

    def h_copy(f):
        return remote(
            hid.at[f + 2], hid.at[f + 2 - frames],
            hd_s.at[f], hd_r.at[f], "tm", nxt,
        )

    def p_copy(f, side):
        if side == 0:
            return remote(gp.at[f, rows], gp.at[f, 0], gp_s.at[f, 0], gp_r.at[f, 0], "height", down)
        return remote(gp.at[f, 1], gp.at[f, rows + 1], gp_s.at[f, 1], gp_r.at[f, 1], "height", up)

    def three(source, f0, f1, f2):
        return jnp.concatenate(
            [source[f].reshape(pix, ch) for f in (f0, f1, f2)], axis=1
        )

    @pl.loop(0, frames)
    def _(step):
        f = frames - 1 - step
        pre = None
        for i in range(3):
            term = dot(
                xs[f, pl.ds(i, rows)].reshape(pix, 3 * ch), ws_ref[i].reshape(3 * ch, ch)
            )
            pre = term if pre is None else pre + term
        sigma = jax.nn.sigmoid(pre)
        hid[f + 2] = (pre * sigma).astype(BF16).reshape(rows, cols, ch)

        @pl.when(jnp.logical_and(f >= frames - 2, has_next))
        def _():
            h_copy(f).start()

        grad_hidden = dot(three(g_ext, f, f + 1, f + 2), wtb[...])
        grad_pre = grad_hidden * sigma * (1.0 + pre * (1.0 - sigma))
        gp[f, pl.ds(1, rows)] = grad_pre.astype(BF16).reshape(rows, cols, ch)
        pl.when(has_down)(p_copy(f, 0).start)
        pl.when(has_up)(p_copy(f, 1).start)
        for r in range(1, rows + 1):
            stack(gp, gps, f, r)

    acc[...] = jnp.zeros((total, ch), F32)

    @pl.loop(0, frames)
    def _(f):
        right = gps[f, pl.ds(1, rows)].reshape(pix, 3 * ch)
        for i in range(3):
            term = tdot(x_ext[f, pl.ds(i, rows)].reshape(pix, ch), right)
            for j in range(3):
                acc[pl.ds((3 * i + j) * ch, ch)] += term[:, (2 - j) * ch : (3 - j) * ch]

    part[pl.ds(0, 9 * ch)] = acc[pl.ds(0, 9 * ch)].astype(BF16)

    def rs1_copy(step):
        peer = lax.rem(me_tm + step, n_tm)
        return peer, remote(
            part.at[pl.ds(pl.multiple_of(peer * chunk, chunk), chunk)], rs1.at[step - 1],
            rs1_s.at[step - 1], rs1_r.at[step - 1], "tm", peer,
        )

    for step in range(1, n_tm):
        peer, copy = rs1_copy(step)
        pl.when(peer < spatial_chunks)(copy.start)

    @pl.when(has_prev)
    def _():
        for f in (frames - 1, frames - 2):
            h_copy(f).wait_recv()

    @pl.loop(0, frames)
    def _(f):
        back = three(hid, f + 2, f + 1, f)
        acc[pl.ds(9 * ch, 3 * ch)] += tdot(back, g_ext[f].reshape(pix, ch))

    part[pl.ds(9 * ch, 3 * ch)] = acc[pl.ds(9 * ch, 3 * ch)].astype(BF16)
    for step in range(1, n_tm):
        peer, copy = rs1_copy(step)
        pl.when(peer >= spatial_chunks)(copy.start)

    @pl.loop(0, frames)
    def _(f):
        mixed = dot(three(hid, f + 2, f + 1, f), wt_ref[...].reshape(3 * ch, ch))
        lo[f] = mixed.astype(BF16).reshape(rows, cols, ch)

    lo_out = pltpu.make_async_copy(lo, lo_hbm.at[0], loc.at[2])
    lo_out.start()

    summed = acc[pl.ds(pl.multiple_of(me_tm * chunk, chunk), chunk)]
    for step in range(1, n_tm):
        rs1_copy(step)[1].wait_recv()
        summed = summed + rs1[step - 1].astype(F32)
    acc[pl.ds(0, chunk)] = summed
    s1[...] = summed.astype(BF16)

    def rs2_copy(step):
        peer = lax.rem(me_h + step, n_h)
        return remote(
            s1.at[pl.ds(pl.multiple_of(peer * piece, piece), piece)], rs2.at[step - 1],
            rs2_s.at[step - 1], rs2_r.at[step - 1], "height", peer,
        )

    for step in range(1, n_h):
        rs2_copy(step).start()

    def gi_copy(f):
        return pltpu.make_async_copy(gi.at[f], gi_hbm.at[0, f], loc.at[3 + f])

    def grad_in(f):
        @pl.when(has_up)
        def _():
            p_copy(f, 0).wait_recv()

        @pl.when(has_down)
        def _():
            p_copy(f, 1).wait_recv()

        for r in (0, rows + 1):
            stack(gp, gps, f, r)
        value = None
        for i in range(3):
            term = dot(gps[f, pl.ds(2 - i, rows)].reshape(pix, 3 * ch), wb[i])
            value = term if value is None else value + term
        gi[f] = value.astype(BF16).reshape(rows, cols, ch)
        gi_copy(f).start()

    pl.loop(frames - 2, frames)(grad_in)

    own = acc[pl.ds(pl.multiple_of(me_h * piece, piece), piece)]
    for step in range(1, n_h):
        rs2_copy(step).wait_recv()
        own = own + rs2[step - 1].astype(F32)
    dps[me_dp] = own

    def dp_copy(step):
        peer = lax.rem(me_dp + step, n_dp)
        return remote(
            dps.at[me_dp], dps.at[me_dp], dp_s.at[step - 1], dp_r.at[me_dp], "dp", peer
        )

    def dp_from(step):
        src = lax.rem(me_dp + n_dp - step, n_dp)
        return remote(dps.at[src], dps.at[src], dp_s.at[step - 1], dp_r.at[src], "dp", src)

    for step in range(1, n_dp):
        dp_copy(step).start()

    pl.loop(0, frames - 2)(grad_in)

    for step in range(1, n_dp):
        dp_from(step).wait_recv()
    whole = dps[0]
    for d in range(1, n_dp):
        whole = whole + dps[d]
    base = pl.multiple_of(me_tm * chunk + me_h * piece, piece)
    res[pl.ds(base, piece)] = (whole * factor).astype(BF16)

    def ag1_copy(step):
        peer = lax.rem(me_h + step, n_h)
        at = res.at[pl.ds(base, piece)]
        return remote(at, at, ag1_s.at[step - 1], ag1_r.at[step - 1], "height", peer)

    def ag1_from(step):
        src = lax.rem(me_h + n_h - step, n_h)
        at = res.at[pl.ds(pl.multiple_of(me_tm * chunk + src * piece, piece), piece)]
        return remote(at, at, ag1_s.at[step - 1], ag1_r.at[step - 1], "height", src)

    for step in range(1, n_h):
        ag1_copy(step).start()
    for step in range(1, n_h):
        ag1_from(step).wait_recv()

    def ag2_copy(step):
        peer = lax.rem(me_tm + step, n_tm)
        at = res.at[pl.ds(pl.multiple_of(me_tm * chunk, chunk), chunk)]
        return remote(at, at, ag2_s.at[step - 1], ag2_r.at[step - 1], "tm", peer)

    def ag2_from(step):
        src = lax.rem(me_tm + n_tm - step, n_tm)
        at = res.at[pl.ds(pl.multiple_of(src * chunk, chunk), chunk)]
        return remote(at, at, ag2_s.at[step - 1], ag2_r.at[step - 1], "tm", src)

    for step in range(1, n_tm):
        ag2_copy(step).start()
    for step in range(1, n_tm):
        ag2_from(step).wait_recv()
    res_out = pltpu.make_async_copy(res, res_hbm, loc.at[3 + frames])
    res_out.start()

    pl.when(has_down)(x_down.wait_send)
    pl.when(has_up)(x_up.wait_send)
    pl.when(has_prev)(g_prev.wait_send)

    @pl.when(has_next)
    def _():
        for f in (frames - 1, frames - 2):
            h_copy(f).wait_send()

    for f in range(frames):
        pl.when(has_down)(p_copy(f, 0).wait_send)
        pl.when(has_up)(p_copy(f, 1).wait_send)
    for step in range(1, n_tm):
        rs1_copy(step)[1].wait_send()
        ag2_copy(step).wait_send()
    for step in range(1, n_h):
        rs2_copy(step).wait_send()
        ag1_copy(step).wait_send()
    for step in range(1, n_dp):
        dp_copy(step).wait_send()
    lo_out.wait()
    for f in range(frames):
        gi_copy(f).wait()
    res_out.wait()


def per_device(sizes, frames_in, grad_out, w_spatial, w_temporal):
    clips, frames, rows, cols, ch = frames_in.shape
    n_dp, n_tm, n_h = sizes
    assert clips == 1 and (12 * ch) % (n_tm * n_h) == 0
    chunk = 12 * ch // n_tm
    piece = chunk // n_h
    factor = 1.0 / math.sqrt(clips * frames * rows * cols * n_dp * n_tm * n_h)
    any_spec = pl.BlockSpec(memory_space=pl.ANY)
    vmem_spec = pl.BlockSpec(memory_space=pltpu.VMEM)
    dma = pltpu.SemaphoreType.DMA
    layer_out, grad_in, sums = pl.pallas_call(
        functools.partial(kernel, sizes, (frames, rows, cols, ch), factor),
        out_shape=(
            jax.ShapeDtypeStruct(frames_in.shape, BF16),
            jax.ShapeDtypeStruct(frames_in.shape, BF16),
            jax.ShapeDtypeStruct((12 * ch, ch), BF16),
        ),
        in_specs=[any_spec, any_spec, vmem_spec, vmem_spec],
        out_specs=(any_spec, any_spec, any_spec),
        scratch_shapes=[
            pltpu.VMEM((frames, rows + 2, cols, ch), BF16),
            pltpu.VMEM((frames, rows + 2, cols, 3 * ch), BF16),
            pltpu.VMEM((frames + 2, rows, cols, ch), BF16),
            pltpu.VMEM((frames + 2, rows, cols, ch), BF16),
            pltpu.VMEM((frames, rows + 2, cols, ch), BF16),
            pltpu.VMEM((frames, rows + 2, cols, 3 * ch), BF16),
            pltpu.VMEM((3, 3 * ch, ch), BF16),
            pltpu.VMEM((3 * ch, ch), BF16),
            pltpu.VMEM((12 * ch, ch), F32),
            pltpu.VMEM((12 * ch, ch), BF16),
            pltpu.VMEM((n_tm - 1, chunk, ch), BF16),
            pltpu.VMEM((chunk, ch), BF16),
            pltpu.VMEM((n_h - 1, piece, ch), BF16),
            pltpu.VMEM((n_dp, piece, ch), F32),
            pltpu.VMEM((12 * ch, ch), BF16),
            pltpu.VMEM((frames, rows, cols, ch), BF16),
            pltpu.VMEM((frames, rows, cols, ch), BF16),
            dma((4 + frames,)),
            dma((2,)), dma((2,)), dma((1,)), dma((1,)),
            dma((frames,)), dma((frames,)), dma((frames, 2)), dma((frames, 2)),
            dma((n_tm - 1,)), dma((n_tm - 1,)), dma((n_h - 1,)), dma((n_h - 1,)),
            dma((n_dp,)), dma((n_dp,)),
            dma((n_h - 1,)), dma((n_h - 1,)), dma((n_tm - 1,)), dma((n_tm - 1,)),
        ],
        compiler_params=pltpu.CompilerParams(
            collective_id=0, has_side_effects=True, vmem_limit_bytes=48 << 20
        ),
    )(frames_in, grad_out, w_spatial, w_temporal)
    sums = sums.astype(F32)
    return (
        layer_out,
        grad_in,
        sums[: 9 * ch].reshape(3, 3, ch, ch),
        sums[9 * ch :].reshape(3, ch, ch),
    )


def solution(mesh):
    sizes = (mesh.shape["dp"], mesh.shape["tm"], mesh.shape["height"])
    spec = P("dp", "tm", "height", None, None)
    return jax.shard_map(
        functools.partial(per_device, sizes), mesh=mesh,
        in_specs=(spec, spec, P(), P()), out_specs=(spec, spec, P(), P()), check_vma=False,
    )
```

```python
import functools
import math

import jax
import jax.numpy as jnp
from jax import lax
from jax.experimental import pallas as pl
from jax.experimental.pallas import tpu as pltpu
from jax.sharding import PartitionSpec as P

F32, BF16 = jnp.float32, jnp.bfloat16


def tdot(lhs, rhs):
    return lax.dot_general(lhs, rhs, (((0,), (0,)), ((), ())), preferred_element_type=F32)


def dot(lhs, rhs):
    return jnp.dot(lhs, rhs, preferred_element_type=F32)


def kernel(
    sizes, dims, factor,
    x_hbm, g_hbm, ws_hbm, wt_hbm,
    lo_hbm, gi_hbm, res_hbm,
    ws_ref, wt_ref, x_ext, xs, g_ext, hid, gp, gps, wb, wtb, acc, part, rs1, s1, rs2, dps, res, lo, gi,
    loc, xh_s, xh_r, gh_s, gh_r, hd_s, hd_r, gp_s, gp_r,
    rs1_s, rs1_r, rs2_s, rs2_r, dp_s, dp_r, ag1_s, ag1_r, ag2_s, ag2_r,
):
    n_dp, n_tm, n_h = sizes
    frames, rows, cols, ch = dims
    pix = rows * cols
    total = 12 * ch
    chunk = total // n_tm
    piece = chunk // n_h
    spatial_chunks = (9 * ch) // chunk
    me_dp, me_tm, me_h = lax.axis_index("dp"), lax.axis_index("tm"), lax.axis_index("height")

    def remote(src, dst, send, recv, axis, peer):
        return pltpu.make_async_remote_copy(
            src_ref=src, dst_ref=dst, send_sem=send, recv_sem=recv,
            device_id={axis: peer}, device_id_type=pl.DeviceIdType.MESH,
        )

    x_in = pltpu.make_async_copy(x_hbm.at[0], x_ext.at[:, pl.ds(1, rows)], loc.at[0])
    g_in = pltpu.make_async_copy(g_hbm.at[0], g_ext.at[pl.ds(0, frames)], loc.at[1])
    ws_in = pltpu.make_async_copy(ws_hbm, ws_ref, loc.at[4 + frames])
    wt_in = pltpu.make_async_copy(wt_hbm, wt_ref, loc.at[5 + frames])
    x_in.start()
    ws_in.start()
    wt_in.start()
    g_in.start()

    barrier = pltpu.get_barrier_semaphore()
    axes = (("dp", n_dp, me_dp), ("tm", n_tm, me_tm), ("height", n_h, me_h))
    for axis, count, me in axes:
        for step in range(1, count):
            pl.semaphore_signal(
                barrier, inc=1, device_id={axis: lax.rem(me + step, count)},
                device_id_type=pl.DeviceIdType.MESH,
            )

    has_up, has_down = me_h > 0, me_h < n_h - 1
    has_prev, has_next = me_tm > 0, me_tm < n_tm - 1
    up, down = lax.rem(me_h + n_h - 1, n_h), lax.rem(me_h + 1, n_h)
    prev, nxt = lax.rem(me_tm + n_tm - 1, n_tm), lax.rem(me_tm + 1, n_tm)

    def x_copy(f, side):
        if side == 0:
            return remote(
                x_hbm.at[0, f, rows - 1], x_ext.at[f, 0],
                xh_s.at[f, 0], xh_r.at[f, 0], "height", down,
            )
        return remote(
            x_hbm.at[0, f, 0], x_ext.at[f, rows + 1],
            xh_s.at[f, 1], xh_r.at[f, 1], "height", up,
        )

    def g_copy(f):
        return remote(g_hbm.at[0, f], g_ext.at[frames + f], gh_s.at[f], gh_r.at[f], "tm", prev)

    @pl.when(me_h == 0)
    def _():
        x_ext[:, 0] = jnp.zeros((frames, cols, ch), BF16)
        gp[:, 0] = jnp.zeros((frames, cols, ch), BF16)

    @pl.when(me_h == n_h - 1)
    def _():
        x_ext[:, rows + 1] = jnp.zeros((frames, cols, ch), BF16)
        gp[:, rows + 1] = jnp.zeros((frames, cols, ch), BF16)

    @pl.when(me_tm == 0)
    def _():
        hid[pl.ds(0, 2)] = jnp.zeros((2, rows, cols, ch), BF16)

    @pl.when(me_tm == n_tm - 1)
    def _():
        g_ext[pl.ds(frames, 2)] = jnp.zeros((2, rows, cols, ch), BF16)

    place = lax.broadcasted_iota(jnp.int32, (cols, ch), 0)

    def stack(source, target, f, r):
        value = source[f, r]
        wide = value.astype(F32)
        left = jnp.where(place == 0, 0.0, pltpu.roll(wide, 1, 0))
        right = jnp.where(place == cols - 1, 0.0, pltpu.roll(wide, cols - 1, 0))
        target[f, r, :, pl.ds(0, ch)] = left.astype(BF16)
        target[f, r, :, pl.ds(ch, ch)] = value
        target[f, r, :, pl.ds(2 * ch, ch)] = right.astype(BF16)

    x_in.wait()

    @pl.loop(0, frames)
    def _(f):
        for r in range(1, rows + 1):
            stack(x_ext, xs, f, r)

    ws_in.wait()
    wt_in.wait()
    for i in range(3):
        for j in range(3):
            wb[i, pl.ds((2 - j) * ch, ch)] = ws_ref[i, j].T
        wtb[pl.ds(i * ch, ch)] = wt_ref[i].T
    g_in.wait()

    pl.semaphore_wait(barrier, n_dp + n_tm + n_h - 3)
    for f in range(frames):
        pl.when(has_down)(x_copy(f, 0).start)
        pl.when(has_up)(x_copy(f, 1).start)
    for f in range(2):
        pl.when(has_prev)(g_copy(f).start)

    def h_copy(f):
        return remote(
            hid.at[f + 2], hid.at[f + 2 - frames],
            hd_s.at[f], hd_r.at[f], "tm", nxt,
        )

    def p_copy(f, side):
        if side == 0:
            return remote(gp.at[f, rows], gp.at[f, 0], gp_s.at[f, 0], gp_r.at[f, 0], "height", down)
        return remote(gp.at[f, 1], gp.at[f, rows + 1], gp_s.at[f, 1], gp_r.at[f, 1], "height", up)

    def three(source, f0, f1, f2):
        return jnp.concatenate(
            [source[f].reshape(pix, ch) for f in (f0, f1, f2)], axis=1
        )

    @pl.loop(0, frames)
    def _(f):
        @pl.when(has_up)
        def _():
            x_copy(f, 0).wait_recv()

        @pl.when(has_down)
        def _():
            x_copy(f, 1).wait_recv()

        for r in (0, rows + 1):
            stack(x_ext, xs, f, r)
        pre = None
        for i in range(3):
            term = dot(
                xs[f, pl.ds(i, rows)].reshape(pix, 3 * ch), ws_ref[i].reshape(3 * ch, ch)
            )
            pre = term if pre is None else pre + term
        sigma = jax.nn.sigmoid(pre)
        hid[f + 2] = (pre * sigma).astype(BF16).reshape(rows, cols, ch)

        @pl.when(jnp.logical_and(f >= frames - 2, has_next))
        def _():
            h_copy(f).start()

        @pl.when(jnp.logical_and(f >= frames - 2, has_next))
        def _():
            g_copy(f + 2 - frames).wait_recv()

        grad_hidden = dot(three(g_ext, f, f + 1, f + 2), wtb[...])
        grad_pre = grad_hidden * sigma * (1.0 + pre * (1.0 - sigma))
        gp[f, pl.ds(1, rows)] = grad_pre.astype(BF16).reshape(rows, cols, ch)
        pl.when(has_down)(p_copy(f, 0).start)
        pl.when(has_up)(p_copy(f, 1).start)
        for r in range(1, rows + 1):
            stack(gp, gps, f, r)

    acc[...] = jnp.zeros((total, ch), F32)

    @pl.loop(0, frames)
    def _(f):
        right = gps[f, pl.ds(1, rows)].reshape(pix, 3 * ch)
        for i in range(3):
            term = tdot(x_ext[f, pl.ds(i, rows)].reshape(pix, ch), right)
            for j in range(3):
                acc[pl.ds((3 * i + j) * ch, ch)] += term[:, (2 - j) * ch : (3 - j) * ch]

    part[pl.ds(0, 9 * ch)] = acc[pl.ds(0, 9 * ch)].astype(BF16)

    def rs1_copy(step):
        peer = lax.rem(me_tm + step, n_tm)
        return peer, remote(
            part.at[pl.ds(pl.multiple_of(peer * chunk, chunk), chunk)], rs1.at[step - 1],
            rs1_s.at[step - 1], rs1_r.at[step - 1], "tm", peer,
        )

    for step in range(1, n_tm):
        peer, copy = rs1_copy(step)
        pl.when(peer < spatial_chunks)(copy.start)

    @pl.when(has_prev)
    def _():
        for f in (frames - 1, frames - 2):
            h_copy(f).wait_recv()

    @pl.loop(0, frames)
    def _(f):
        back = three(hid, f + 2, f + 1, f)
        acc[pl.ds(9 * ch, 3 * ch)] += tdot(back, g_ext[f].reshape(pix, ch))

    part[pl.ds(9 * ch, 3 * ch)] = acc[pl.ds(9 * ch, 3 * ch)].astype(BF16)
    for step in range(1, n_tm):
        peer, copy = rs1_copy(step)
        pl.when(peer >= spatial_chunks)(copy.start)

    @pl.loop(0, frames)
    def _(f):
        mixed = dot(three(hid, f + 2, f + 1, f), wt_ref[...].reshape(3 * ch, ch))
        lo[f] = mixed.astype(BF16).reshape(rows, cols, ch)

    lo_out = pltpu.make_async_copy(lo, lo_hbm.at[0], loc.at[2])
    lo_out.start()

    summed = acc[pl.ds(pl.multiple_of(me_tm * chunk, chunk), chunk)]
    for step in range(1, n_tm):
        rs1_copy(step)[1].wait_recv()
        summed = summed + rs1[step - 1].astype(F32)
    acc[pl.ds(0, chunk)] = summed
    s1[...] = summed.astype(BF16)

    def rs2_copy(step):
        peer = lax.rem(me_h + step, n_h)
        return remote(
            s1.at[pl.ds(pl.multiple_of(peer * piece, piece), piece)], rs2.at[step - 1],
            rs2_s.at[step - 1], rs2_r.at[step - 1], "height", peer,
        )

    for step in range(1, n_h):
        rs2_copy(step).start()

    def gi_copy(f):
        return pltpu.make_async_copy(gi.at[f], gi_hbm.at[0, f], loc.at[3 + f])

    def grad_in(f):
        @pl.when(has_up)
        def _():
            p_copy(f, 0).wait_recv()

        @pl.when(has_down)
        def _():
            p_copy(f, 1).wait_recv()

        for r in (0, rows + 1):
            stack(gp, gps, f, r)
        value = None
        for i in range(3):
            term = dot(gps[f, pl.ds(2 - i, rows)].reshape(pix, 3 * ch), wb[i])
            value = term if value is None else value + term
        gi[f] = value.astype(BF16).reshape(rows, cols, ch)
        gi_copy(f).start()

    pl.loop(0, 2)(grad_in)

    own = acc[pl.ds(pl.multiple_of(me_h * piece, piece), piece)]
    for step in range(1, n_h):
        rs2_copy(step).wait_recv()
        own = own + rs2[step - 1].astype(F32)
    dps[me_dp] = own

    def dp_copy(step):
        peer = lax.rem(me_dp + step, n_dp)
        return remote(
            dps.at[me_dp], dps.at[me_dp], dp_s.at[step - 1], dp_r.at[me_dp], "dp", peer
        )

    def dp_from(step):
        src = lax.rem(me_dp + n_dp - step, n_dp)
        return remote(dps.at[src], dps.at[src], dp_s.at[step - 1], dp_r.at[src], "dp", src)

    for step in range(1, n_dp):
        dp_copy(step).start()

    pl.loop(2, frames)(grad_in)

    for step in range(1, n_dp):
        dp_from(step).wait_recv()
    whole = dps[0]
    for d in range(1, n_dp):
        whole = whole + dps[d]
    base = pl.multiple_of(me_tm * chunk + me_h * piece, piece)
    res[pl.ds(base, piece)] = (whole * factor).astype(BF16)

    def ag1_copy(step):
        peer = lax.rem(me_h + step, n_h)
        at = res.at[pl.ds(base, piece)]
        return remote(at, at, ag1_s.at[step - 1], ag1_r.at[step - 1], "height", peer)

    def ag1_from(step):
        src = lax.rem(me_h + n_h - step, n_h)
        at = res.at[pl.ds(pl.multiple_of(me_tm * chunk + src * piece, piece), piece)]
        return remote(at, at, ag1_s.at[step - 1], ag1_r.at[step - 1], "height", src)

    far, near = lax.rem(me_tm + n_tm // 2, n_tm), me_tm + 1 - 2 * lax.rem(me_tm, 2)

    def at_piece(tm, height):
        return res.at[pl.ds(pl.multiple_of(tm * chunk + height * piece, piece), piece)]

    def ag2_copy(tm, step, kind):
        at = at_piece(tm, lax.rem(me_h + n_h - step, n_h))
        return remote(
            at, at, ag2_s.at[kind, step], ag2_r.at[kind, step], "tm", far if kind == 0 else near
        )

    for step in range(1, n_h):
        ag1_copy(step).start()
    for step in range(n_h):
        if step > 0:
            ag1_from(step).wait_recv()
        ag2_copy(me_tm, step, 0).start()
        ag2_copy(me_tm, step, 1).start()
    for step in range(n_h):
        ag2_copy(far, step, 0).wait_recv()
        ag2_copy(far, step, 2).start()
    for step in range(n_h):
        ag2_copy(near, step, 1).wait_recv()
        ag2_copy(near, step, 2).wait_recv()
    res_out = pltpu.make_async_copy(res, res_hbm, loc.at[3 + frames])
    res_out.start()

    for f in range(frames):
        pl.when(has_down)(x_copy(f, 0).wait_send)
        pl.when(has_up)(x_copy(f, 1).wait_send)
    for f in range(2):
        pl.when(has_prev)(g_copy(f).wait_send)

    @pl.when(has_next)
    def _():
        for f in (frames - 1, frames - 2):
            h_copy(f).wait_send()

    for f in range(frames):
        pl.when(has_down)(p_copy(f, 0).wait_send)
        pl.when(has_up)(p_copy(f, 1).wait_send)
    for step in range(1, n_tm):
        rs1_copy(step)[1].wait_send()
    for step in range(n_h):
        for kind in range(3):
            ag2_copy(me_tm, step, kind).wait_send()
    for step in range(1, n_h):
        rs2_copy(step).wait_send()
        ag1_copy(step).wait_send()
    for step in range(1, n_dp):
        dp_copy(step).wait_send()
    lo_out.wait()
    for f in range(frames):
        gi_copy(f).wait()
    res_out.wait()


def per_device(sizes, frames_in, grad_out, w_spatial, w_temporal):
    clips, frames, rows, cols, ch = frames_in.shape
    n_dp, n_tm, n_h = sizes
    assert clips == 1 and n_tm == 4 and frames > 2 and (12 * ch) % (n_tm * n_h) == 0
    chunk = 12 * ch // n_tm
    piece = chunk // n_h
    factor = 1.0 / math.sqrt(clips * frames * rows * cols * n_dp * n_tm * n_h)
    any_spec = pl.BlockSpec(memory_space=pl.ANY)
    dma = pltpu.SemaphoreType.DMA
    layer_out, grad_in, sums = pl.pallas_call(
        functools.partial(kernel, sizes, (frames, rows, cols, ch), factor),
        out_shape=(
            jax.ShapeDtypeStruct(frames_in.shape, BF16),
            jax.ShapeDtypeStruct(frames_in.shape, BF16),
            jax.ShapeDtypeStruct((12 * ch, ch), BF16),
        ),
        in_specs=[any_spec] * 4,
        out_specs=(any_spec, any_spec, any_spec),
        scratch_shapes=[
            pltpu.VMEM((3, 3, ch, ch), BF16),
            pltpu.VMEM((3, ch, ch), BF16),
            pltpu.VMEM((frames, rows + 2, cols, ch), BF16),
            pltpu.VMEM((frames, rows + 2, cols, 3 * ch), BF16),
            pltpu.VMEM((frames + 2, rows, cols, ch), BF16),
            pltpu.VMEM((frames + 2, rows, cols, ch), BF16),
            pltpu.VMEM((frames, rows + 2, cols, ch), BF16),
            pltpu.VMEM((frames, rows + 2, cols, 3 * ch), BF16),
            pltpu.VMEM((3, 3 * ch, ch), BF16),
            pltpu.VMEM((3 * ch, ch), BF16),
            pltpu.VMEM((12 * ch, ch), F32),
            pltpu.VMEM((12 * ch, ch), BF16),
            pltpu.VMEM((n_tm - 1, chunk, ch), BF16),
            pltpu.VMEM((chunk, ch), BF16),
            pltpu.VMEM((n_h - 1, piece, ch), BF16),
            pltpu.VMEM((n_dp, piece, ch), F32),
            pltpu.VMEM((12 * ch, ch), BF16),
            pltpu.VMEM((frames, rows, cols, ch), BF16),
            pltpu.VMEM((frames, rows, cols, ch), BF16),
            dma((6 + frames,)),
            dma((frames, 2)), dma((frames, 2)), dma((2,)), dma((2,)),
            dma((frames,)), dma((frames,)), dma((frames, 2)), dma((frames, 2)),
            dma((n_tm - 1,)), dma((n_tm - 1,)), dma((n_h - 1,)), dma((n_h - 1,)),
            dma((n_dp,)), dma((n_dp,)),
            dma((n_h - 1,)), dma((n_h - 1,)), dma((3, n_h)), dma((3, n_h)),
        ],
        compiler_params=pltpu.CompilerParams(
            collective_id=0, has_side_effects=True, vmem_limit_bytes=63 << 20
        ),
    )(frames_in, grad_out, w_spatial, w_temporal)
    sums = sums.astype(F32)
    return (
        layer_out,
        grad_in,
        sums[: 9 * ch].reshape(3, 3, ch, ch),
        sums[9 * ch :].reshape(3, ch, ch),
    )


def solution(mesh):
    sizes = (mesh.shape["dp"], mesh.shape["tm"], mesh.shape["height"])
    spec = P("dp", "tm", "height", None, None)
    return jax.shard_map(
        functools.partial(per_device, sizes), mesh=mesh,
        in_specs=(spec, spec, P(), P()), out_specs=(spec, spec, P(), P()), check_vma=False,
    )
```

```python
import functools
import math

import jax
import jax.numpy as jnp
from jax import lax
from jax.experimental import pallas as pl
from jax.experimental.pallas import tpu as pltpu
from jax.sharding import PartitionSpec as P

F32, BF16 = jnp.float32, jnp.bfloat16


def tdot(lhs, rhs):
    return lax.dot_general(lhs, rhs, (((0,), (0,)), ((), ())), preferred_element_type=F32)


def dot(lhs, rhs):
    return jnp.dot(lhs, rhs, preferred_element_type=F32)


def kernel(
    sizes, dims, factor,
    x_hbm, g_hbm, ws_hbm, wt_hbm,
    lo_hbm, gi_hbm, res_hbm,
    ws_ref, wt_ref, x_ext, xs, g_ext, hid, gp, gps, wb, wtb, acc, part, rs1, s1, rs2, dps, res, lo, gi,
    loc, xh_s, xh_r, gh_s, gh_r, hd_s, hd_r, gp_s, gp_r,
    rs1_s, rs1_r, rs2_s, rs2_r, dp_s, dp_r, ag1_s, ag1_r, ag2_s, ag2_r,
):
    n_dp, n_tm, n_h = sizes
    frames, rows, cols, ch = dims
    pix = rows * cols
    total = 12 * ch
    chunk = total // n_tm
    piece = chunk // n_h
    spatial_chunks = (9 * ch) // chunk
    me_dp, me_tm, me_h = lax.axis_index("dp"), lax.axis_index("tm"), lax.axis_index("height")

    def remote(src, dst, send, recv, axis, peer):
        return pltpu.make_async_remote_copy(
            src_ref=src, dst_ref=dst, send_sem=send, recv_sem=recv,
            device_id={axis: peer}, device_id_type=pl.DeviceIdType.MESH,
        )

    x_in = pltpu.make_async_copy(x_hbm.at[0], x_ext.at[:, pl.ds(1, rows)], loc.at[0])
    g_in = pltpu.make_async_copy(g_hbm.at[0], g_ext.at[pl.ds(0, frames)], loc.at[1])
    ws_in = pltpu.make_async_copy(ws_hbm, ws_ref, loc.at[4 + frames])
    wt_in = pltpu.make_async_copy(wt_hbm, wt_ref, loc.at[5 + frames])
    x_in.start()
    ws_in.start()
    wt_in.start()
    g_in.start()

    barrier = pltpu.get_barrier_semaphore()
    axes = (("dp", n_dp, me_dp), ("tm", n_tm, me_tm), ("height", n_h, me_h))
    for axis, count, me in axes:
        for step in range(1, count):
            pl.semaphore_signal(
                barrier, inc=1, device_id={axis: lax.rem(me + step, count)},
                device_id_type=pl.DeviceIdType.MESH,
            )

    has_up, has_down = me_h > 0, me_h < n_h - 1
    has_prev, has_next = me_tm > 0, me_tm < n_tm - 1
    up, down = lax.rem(me_h + n_h - 1, n_h), lax.rem(me_h + 1, n_h)
    prev, nxt = lax.rem(me_tm + n_tm - 1, n_tm), lax.rem(me_tm + 1, n_tm)

    def x_copy(f, side):
        if side == 0:
            return remote(
                x_hbm.at[0, f, rows - 1], x_ext.at[f, 0],
                xh_s.at[f, 0], xh_r.at[f, 0], "height", down,
            )
        return remote(
            x_hbm.at[0, f, 0], x_ext.at[f, rows + 1],
            xh_s.at[f, 1], xh_r.at[f, 1], "height", up,
        )

    def g_copy(f):
        return remote(g_hbm.at[0, f], g_ext.at[frames + f], gh_s.at[f], gh_r.at[f], "tm", prev)

    @pl.when(me_h == 0)
    def _():
        x_ext[:, 0] = jnp.zeros((frames, cols, ch), BF16)
        gp[:, 0] = jnp.zeros((frames, cols, ch), BF16)

    @pl.when(me_h == n_h - 1)
    def _():
        x_ext[:, rows + 1] = jnp.zeros((frames, cols, ch), BF16)
        gp[:, rows + 1] = jnp.zeros((frames, cols, ch), BF16)

    @pl.when(me_tm == 0)
    def _():
        hid[pl.ds(0, 2)] = jnp.zeros((2, rows, cols, ch), BF16)

    @pl.when(me_tm == n_tm - 1)
    def _():
        g_ext[pl.ds(frames, 2)] = jnp.zeros((2, rows, cols, ch), BF16)

    place = lax.broadcasted_iota(jnp.int32, (cols, ch), 0)

    def stack(source, target, f, r):
        value = source[f, r]
        wide = value.astype(F32)
        left = jnp.where(place == 0, 0.0, pltpu.roll(wide, 1, 0))
        right = jnp.where(place == cols - 1, 0.0, pltpu.roll(wide, cols - 1, 0))
        target[f, r, :, pl.ds(0, ch)] = left.astype(BF16)
        target[f, r, :, pl.ds(ch, ch)] = value
        target[f, r, :, pl.ds(2 * ch, ch)] = right.astype(BF16)

    x_in.wait()

    @pl.loop(0, frames)
    def _(f):
        for r in range(1, rows + 1):
            stack(x_ext, xs, f, r)

    ws_in.wait()
    wt_in.wait()
    for i in range(3):
        for j in range(3):
            wb[i, pl.ds((2 - j) * ch, ch)] = ws_ref[i, j].T
        wtb[pl.ds(i * ch, ch)] = wt_ref[i].T
    g_in.wait()

    pl.semaphore_wait(barrier, n_dp + n_tm + n_h - 3)
    for f in range(frames):
        pl.when(has_down)(x_copy(f, 0).start)
        pl.when(has_up)(x_copy(f, 1).start)
    for f in range(2):
        pl.when(has_prev)(g_copy(f).start)

    def h_copy(f):
        return remote(
            hid.at[f + 2], hid.at[f + 2 - frames],
            hd_s.at[f], hd_r.at[f], "tm", nxt,
        )

    def p_copy(f, side):
        if side == 0:
            return remote(gp.at[f, rows], gp.at[f, 0], gp_s.at[f, 0], gp_r.at[f, 0], "height", down)
        return remote(gp.at[f, 1], gp.at[f, rows + 1], gp_s.at[f, 1], gp_r.at[f, 1], "height", up)

    def three(source, f0, f1, f2):
        return jnp.concatenate(
            [source[f].reshape(pix, ch) for f in (f0, f1, f2)], axis=1
        )

    @pl.loop(0, frames)
    def _(f):
        @pl.when(has_up)
        def _():
            x_copy(f, 0).wait_recv()

        @pl.when(has_down)
        def _():
            x_copy(f, 1).wait_recv()

        for r in (0, rows + 1):
            stack(x_ext, xs, f, r)
        pre = None
        for i in range(3):
            term = dot(
                xs[f, pl.ds(i, rows)].reshape(pix, 3 * ch), ws_ref[i].reshape(3 * ch, ch)
            )
            pre = term if pre is None else pre + term
        sigma = jax.nn.sigmoid(pre)
        hid[f + 2] = (pre * sigma).astype(BF16).reshape(rows, cols, ch)

        @pl.when(jnp.logical_and(f >= frames - 2, has_next))
        def _():
            h_copy(f).start()

        @pl.when(jnp.logical_and(f >= frames - 2, has_next))
        def _():
            g_copy(f + 2 - frames).wait_recv()

        grad_hidden = dot(three(g_ext, f, f + 1, f + 2), wtb[...])
        grad_pre = grad_hidden * sigma * (1.0 + pre * (1.0 - sigma))
        gp[f, pl.ds(1, rows)] = grad_pre.astype(BF16).reshape(rows, cols, ch)
        pl.when(has_down)(p_copy(f, 0).start)
        pl.when(has_up)(p_copy(f, 1).start)
        for r in range(1, rows + 1):
            stack(gp, gps, f, r)

    acc[...] = jnp.zeros((total, ch), F32)

    @pl.loop(0, frames)
    def _(f):
        right = gps[f, pl.ds(1, rows)].reshape(pix, 3 * ch)
        for i in range(3):
            term = tdot(x_ext[f, pl.ds(i, rows)].reshape(pix, ch), right)
            for j in range(3):
                acc[pl.ds((3 * i + j) * ch, ch)] += term[:, (2 - j) * ch : (3 - j) * ch]

    part[pl.ds(0, 9 * ch)] = acc[pl.ds(0, 9 * ch)].astype(BF16)

    def rs1_copy(step):
        peer = lax.rem(me_tm + step, n_tm)
        return peer, remote(
            part.at[pl.ds(pl.multiple_of(peer * chunk, chunk), chunk)], rs1.at[step - 1],
            rs1_s.at[step - 1], rs1_r.at[step - 1], "tm", peer,
        )

    for step in range(1, n_tm):
        peer, copy = rs1_copy(step)
        pl.when(peer < spatial_chunks)(copy.start)

    @pl.when(has_prev)
    def _():
        for f in (frames - 1, frames - 2):
            h_copy(f).wait_recv()

    @pl.loop(0, frames)
    def _(f):
        back = three(hid, f + 2, f + 1, f)
        acc[pl.ds(9 * ch, 3 * ch)] += tdot(back, g_ext[f].reshape(pix, ch))

    part[pl.ds(9 * ch, 3 * ch)] = acc[pl.ds(9 * ch, 3 * ch)].astype(BF16)
    for step in range(1, n_tm):
        peer, copy = rs1_copy(step)
        pl.when(peer >= spatial_chunks)(copy.start)

    @pl.loop(0, frames)
    def _(f):
        mixed = dot(three(hid, f + 2, f + 1, f), wt_ref[...].reshape(3 * ch, ch))
        lo[f] = mixed.astype(BF16).reshape(rows, cols, ch)

    lo_out = pltpu.make_async_copy(lo, lo_hbm.at[0], loc.at[2])
    lo_out.start()

    summed = acc[pl.ds(pl.multiple_of(me_tm * chunk, chunk), chunk)]
    for step in range(1, n_tm):
        rs1_copy(step)[1].wait_recv()
        summed = summed + rs1[step - 1].astype(F32)
    acc[pl.ds(0, chunk)] = summed
    s1[...] = summed.astype(BF16)

    def rs2_copy(step):
        peer = lax.rem(me_h + step, n_h)
        return remote(
            s1.at[pl.ds(pl.multiple_of(peer * piece, piece), piece)], rs2.at[step - 1],
            rs2_s.at[step - 1], rs2_r.at[step - 1], "height", peer,
        )

    for step in range(1, n_h):
        rs2_copy(step).start()

    def gi_copy(f):
        return pltpu.make_async_copy(gi.at[f], gi_hbm.at[0, f], loc.at[3 + f])

    def grad_in(f):
        @pl.when(has_up)
        def _():
            p_copy(f, 0).wait_recv()

        @pl.when(has_down)
        def _():
            p_copy(f, 1).wait_recv()

        for r in (0, rows + 1):
            stack(gp, gps, f, r)
        value = None
        for i in range(3):
            term = dot(gps[f, pl.ds(2 - i, rows)].reshape(pix, 3 * ch), wb[i])
            value = term if value is None else value + term
        gi[f] = value.astype(BF16).reshape(rows, cols, ch)
        gi_copy(f).start()

    pl.loop(0, 2)(grad_in)

    own = acc[pl.ds(pl.multiple_of(me_h * piece, piece), piece)]
    for step in range(1, n_h):
        rs2_copy(step).wait_recv()
        own = own + rs2[step - 1].astype(F32)
    dps[me_dp] = own

    def dp_copy(step):
        peer = lax.rem(me_dp + step, n_dp)
        return remote(
            dps.at[me_dp], dps.at[me_dp], dp_s.at[step - 1], dp_r.at[me_dp], "dp", peer
        )

    def dp_from(step):
        src = lax.rem(me_dp + n_dp - step, n_dp)
        return remote(dps.at[src], dps.at[src], dp_s.at[step - 1], dp_r.at[src], "dp", src)

    for step in range(1, n_dp):
        dp_copy(step).start()

    pl.loop(2, frames)(grad_in)

    for step in range(1, n_dp):
        dp_from(step).wait_recv()
    whole = dps[0]
    for d in range(1, n_dp):
        whole = whole + dps[d]
    base = pl.multiple_of(me_tm * chunk + me_h * piece, piece)
    res[pl.ds(base, piece)] = (whole * factor).astype(BF16)

    def ag1_copy(step):
        peer = lax.rem(me_h + step, n_h)
        at = res.at[pl.ds(base, piece)]
        return remote(at, at, ag1_s.at[step - 1], ag1_r.at[step - 1], "height", peer)

    def ag1_from(step):
        src = lax.rem(me_h + n_h - step, n_h)
        at = res.at[pl.ds(pl.multiple_of(me_tm * chunk + src * piece, piece), piece)]
        return remote(at, at, ag1_s.at[step - 1], ag1_r.at[step - 1], "height", src)

    far, near = lax.rem(me_tm + n_tm // 2, n_tm), me_tm + 1 - 2 * lax.rem(me_tm, 2)

    def at_piece(tm, height):
        return res.at[pl.ds(pl.multiple_of(tm * chunk + height * piece, piece), piece)]

    def ag2_copy(tm, step, kind):
        at = at_piece(tm, lax.rem(me_h + n_h - step, n_h))
        return remote(
            at, at, ag2_s.at[kind, step], ag2_r.at[kind, step], "tm", far if kind == 0 else near
        )

    for step in range(1, n_h):
        ag1_copy(step).start()
    for step in range(n_h):
        if step > 0:
            ag1_from(step).wait_recv()
        ag2_copy(me_tm, step, 0).start()
        ag2_copy(me_tm, step, 1).start()
    for step in range(n_h):
        ag2_copy(far, step, 0).wait_recv()
        ag2_copy(far, step, 2).start()
    for step in range(n_h):
        ag2_copy(near, step, 1).wait_recv()
        ag2_copy(near, step, 2).wait_recv()
    res_out = pltpu.make_async_copy(res, res_hbm, loc.at[3 + frames])
    res_out.start()

    for f in range(frames):
        pl.when(has_down)(x_copy(f, 0).wait_send)
        pl.when(has_up)(x_copy(f, 1).wait_send)
    for f in range(2):
        pl.when(has_prev)(g_copy(f).wait_send)

    @pl.when(has_next)
    def _():
        for f in (frames - 1, frames - 2):
            h_copy(f).wait_send()

    for f in range(frames):
        pl.when(has_down)(p_copy(f, 0).wait_send)
        pl.when(has_up)(p_copy(f, 1).wait_send)
    for step in range(1, n_tm):
        rs1_copy(step)[1].wait_send()
    for step in range(n_h):
        for kind in range(3):
            ag2_copy(me_tm, step, kind).wait_send()
    for step in range(1, n_h):
        rs2_copy(step).wait_send()
        ag1_copy(step).wait_send()
    for step in range(1, n_dp):
        dp_copy(step).wait_send()
    lo_out.wait()
    for f in range(frames):
        gi_copy(f).wait()
    res_out.wait()


def per_device(sizes, frames_in, grad_out, w_spatial, w_temporal):
    clips, frames, rows, cols, ch = frames_in.shape
    n_dp, n_tm, n_h = sizes
    assert clips == 1 and n_tm == 4 and frames > 2 and (12 * ch) % (n_tm * n_h) == 0
    chunk = 12 * ch // n_tm
    piece = chunk // n_h
    factor = 1.0 / math.sqrt(clips * frames * rows * cols * n_dp * n_tm * n_h)
    operands = [
        pltpu.with_memory_space_constraint(a, pltpu.HBM)
        for a in (frames_in, grad_out, w_spatial, w_temporal)
    ]
    any_spec = pl.BlockSpec(memory_space=pl.ANY)
    dma = pltpu.SemaphoreType.DMA
    layer_out, grad_in, sums = pl.pallas_call(
        functools.partial(kernel, sizes, (frames, rows, cols, ch), factor),
        out_shape=(
            jax.ShapeDtypeStruct(frames_in.shape, BF16),
            jax.ShapeDtypeStruct(frames_in.shape, BF16),
            jax.ShapeDtypeStruct((12 * ch, ch), BF16),
        ),
        in_specs=[any_spec] * 4,
        out_specs=(any_spec, any_spec, any_spec),
        scratch_shapes=[
            pltpu.VMEM((3, 3, ch, ch), BF16),
            pltpu.VMEM((3, ch, ch), BF16),
            pltpu.VMEM((frames, rows + 2, cols, ch), BF16),
            pltpu.VMEM((frames, rows + 2, cols, 3 * ch), BF16),
            pltpu.VMEM((frames + 2, rows, cols, ch), BF16),
            pltpu.VMEM((frames + 2, rows, cols, ch), BF16),
            pltpu.VMEM((frames, rows + 2, cols, ch), BF16),
            pltpu.VMEM((frames, rows + 2, cols, 3 * ch), BF16),
            pltpu.VMEM((3, 3 * ch, ch), BF16),
            pltpu.VMEM((3 * ch, ch), BF16),
            pltpu.VMEM((12 * ch, ch), F32),
            pltpu.VMEM((12 * ch, ch), BF16),
            pltpu.VMEM((n_tm - 1, chunk, ch), BF16),
            pltpu.VMEM((chunk, ch), BF16),
            pltpu.VMEM((n_h - 1, piece, ch), BF16),
            pltpu.VMEM((n_dp, piece, ch), F32),
            pltpu.VMEM((12 * ch, ch), BF16),
            pltpu.VMEM((frames, rows, cols, ch), BF16),
            pltpu.VMEM((frames, rows, cols, ch), BF16),
            dma((6 + frames,)),
            dma((frames, 2)), dma((frames, 2)), dma((2,)), dma((2,)),
            dma((frames,)), dma((frames,)), dma((frames, 2)), dma((frames, 2)),
            dma((n_tm - 1,)), dma((n_tm - 1,)), dma((n_h - 1,)), dma((n_h - 1,)),
            dma((n_dp,)), dma((n_dp,)),
            dma((n_h - 1,)), dma((n_h - 1,)), dma((3, n_h)), dma((3, n_h)),
        ],
        compiler_params=pltpu.CompilerParams(
            collective_id=0, has_side_effects=True, vmem_limit_bytes=48 << 20
        ),
    )(*operands)
    sums = sums.astype(F32)
    return (
        layer_out,
        grad_in,
        sums[: 9 * ch].reshape(3, 3, ch, ch),
        sums[9 * ch :].reshape(3, ch, ch),
    )


def solution(mesh):
    sizes = (mesh.shape["dp"], mesh.shape["tm"], mesh.shape["height"])
    spec = P("dp", "tm", "height", None, None)
    return jax.shard_map(
        functools.partial(per_device, sizes), mesh=mesh,
        in_specs=(spec, spec, P(), P()), out_specs=(spec, spec, P(), P()), check_vma=False,
    )
```
